32 devices in a mesh: dp: 8 (over z, x), tensor: 4 (over y, core).
Axes of the slice: x: 2, y: 2, z: 4, core: 2. Of those that a mesh axis runs over, the one named last changes fastest.
Arguments:
- x_in: float32 [8, 1024, 2048], P('dp', 'tensor'), may hold values from -6 to 6
- segments: int32 [8, 1024], P('dp'), may hold values from 0 to 6, as said below
- positions: int32 [8, 1024], P('dp'), may hold values from 0 to 2046, as said below
- ln_gain: float32 [2048], replicated, may hold values from 0.5 to 1.5
- ln_bias: float32 [2048], replicated, may hold values from -3 to 3
- w_qkv: bfloat16 [2048, 3, 2048], P('dp', None, 'tensor')
- b_qkv: float32 [3, 2048], P(None, 'tensor'), may hold values from -3 to 3
- w_out: bfloat16 [2048, 2048], P('tensor', 'dp'), may hold values from -0.5 to 0.5
- w_up: bfloat16 [2048, 8192], P('dp', 'tensor'), may hold values from -0.125 to 0.125
- b_up: float32 [8192], P('tensor'), may hold values from -3 to 3
- w_down: bfloat16 [8192, 2048], P('tensor', 'dp'), may hold values from -0.0625 to 0.0625
- b_out: float32 [2048], replicated, may hold values from -3 to 3
- cotangent: float32 [8, 1024, 2048], P('dp', 'tensor'), may hold values from -6 to 6
Outputs:
- result: float32 [8, 1024, 2048], P('dp', 'tensor')
- x_grad: float32 [8, 1024, 2048], P('dp', 'tensor')
- g_ln_gain: float32 [2048], replicated
- g_ln_bias: float32 [2048], replicated
- g_w_qkv: float32 [2048, 3, 2048], P('dp', None, 'tensor')
- g_b_qkv: float32 [3, 2048], P(None, 'tensor')
- g_w_out: float32 [2048, 2048], P('tensor', 'dp')
- g_w_up: float32 [2048, 8192], P('dp', 'tensor')
- g_b_up: float32 [8192], P('tensor')
- g_w_down: float32 [8192, 2048], P('tensor', 'dp')
- g_b_out: float32 [2048], replicated
The draws below stay inside these ranges and needn't reach their ends.
Inputs may be any that keep to these rules, and one draw needn't show every extreme that they name: `segments`: segment numbers start at 0 at each sequence's first token, never fall along a sequence, and rise by one where a new document starts. `positions`: a token's position counted from its document's start; it rises by one from token to token within a document, and a sequence's first document may have begun before the sequence.
All inputs are finite; a program needn't handle non-finite values.
Results may differ from the reference program's by a relative error of at most 0.013.
Values may be sent and summed in bfloat16 or wider, within the bound.
No kernel may reach another device: no remote copies, remote signals or barrier semaphores. Data moves between devices by JAX's collectives and lax.ppermute only.
A program may use at most 256 MiB of HBM per device.

```python
from functools import partial
import jax
import jax.numpy as jnp
from jax import lax

D = 2048
H = 32
HD = 64
ROT = 32
FF = 8192
LEN = 1024
SEQS = 8


def doc_layout(key):
    base = jax.random.fold_in(key, 7)
    first_key, second_key = jax.random.split(base)
    count = 7
    fifth = LEN // 5
    doc_lengths = jax.random.randint(first_key, (SEQS, count), fifth, 2 * LEN)
    offsets = jax.random.randint(second_key, (SEQS, 1), 0, doc_lengths[:, :1])
    rows = jnp.arange(SEQS, dtype=jnp.int32)[:, None]
    columns = jnp.arange(count, dtype=jnp.int32)[None, :]
    doc_lengths = jnp.where(rows == 0, fifth, doc_lengths)
    offsets = jnp.where(rows[:, :1] == 0, fifth - 1, offsets)
    longest = jnp.where(columns == 0, 2 * LEN - 1, doc_lengths)
    doc_lengths = jnp.where(rows == 1, longest, doc_lengths)
    offsets = jnp.where(rows[:, :1] == 1, LEN - 1, offsets)
    ends = jnp.cumsum(doc_lengths, axis=1) - offsets
    starts = ends - doc_lengths
    places = jnp.arange(LEN, dtype=jnp.int32)
    segment = jnp.sum((ends[:, None, :] <= places[None, :, None]).astype(jnp.int32), axis=2)
    onehot = (segment[:, :, None] == jnp.arange(count, dtype=jnp.int32)[None, None, :]).astype(jnp.int32)
    start_here = jnp.sum(onehot * starts[:, None, :], axis=2)
    return (segment.astype(jnp.int32), (places[None, :] - start_here).astype(jnp.int32))


def draw_segments(key, part):
    return doc_layout(key)[0]


def draw_positions(key, part):
    return doc_layout(key)[1]


def draw_w_qkv(key, part):
    base = jax.random.normal(jax.random.fold_in(key, 11), (D, 3, D), jnp.float32) * D ** (-0.5)
    return base.astype(jnp.bfloat16)


def with_spikes(drawn, stream_key, source, target, shards_of, factor):
    owner, partner = [(jnp.arange(drawn.shape[position]) // (drawn.shape[position] // shards_of)).reshape([-1 if axis == position else 1 for axis in range(drawn.ndim)]) for position in (source, target)]
    chosen = jax.random.permutation(stream_key, shards_of)[partner]
    strong = (owner == chosen) | (owner == (partner + shards_of // 2) % shards_of)
    return jnp.where(strong, factor * drawn, drawn)


def levels(rng, dims, cuts, low, high):
    level, own = 1.0, jax.random.fold_in(rng, 6)
    for axis_at, parts in cuts:
        heights = jnp.exp(jax.random.uniform(jax.random.fold_in(own, axis_at), (parts,), jnp.float32, low / len(cuts), high / len(cuts)))
        level = level * jnp.repeat(heights, dims[axis_at] // parts).reshape([-1 if axis == axis_at else 1 for axis in range(len(dims))])
    return level


def bell_draw(rng, dims, spread, reach, cuts=(), kind=jnp.bfloat16):
    array = jax.random.normal(rng, dims, jnp.float32) * spread
    if len(cuts) > 0:
        array = levels(rng, dims, cuts, -0.22, 0.18) * array
    return jnp.clip(array, min=-reach, max=reach).astype(kind)


def noise_with(rng, dims, spread, limit, cuts, heavy, held_as=jnp.bfloat16):
    values = spread * jax.random.normal(rng, dims, jnp.float32)
    if cuts:
        values = values * levels(rng, dims, cuts, -0.22, 0.18)
    return jnp.clip(with_spikes(values, jax.random.fold_in(rng, 3), *heavy), -limit, limit).astype(held_as)


def setup_inputs(seed: int = 0) -> dict:
    key_list = jax.random.split(jax.random.key(seed), 14)
    x_in = bell_draw(key_list[0], (SEQS, LEN, D), 1.0, 6.0, ((0, 8), (1, 4)), jnp.float32)
    segments = draw_segments(jax.random.fold_in(key_list[13], 71), 0)
    positions = draw_positions(jax.random.fold_in(key_list[13], 71), 0)
    ln_gain = jnp.clip(1.0 + 0.1 * jax.random.normal(key_list[3], (D,), jnp.float32), 0.5, 1.5)
    ln_bias = bell_draw(key_list[4], (D,), 0.5, 3.0, (), jnp.float32)
    w_qkv = draw_w_qkv(jax.random.fold_in(key_list[13], 71), 0)
    b_qkv = bell_draw(key_list[6], (3, D), 0.5, 3.0, ((1, 4),), jnp.float32)
    w_out = bell_draw(key_list[7], (D, D), (D // 16) ** -0.5, 0.5, ((0, 4), (1, 8)))
    w_up = bell_draw(key_list[8], (D, FF), D ** -0.5, 0.125, ((0, 8), (1, 4)))
    b_up = bell_draw(key_list[9], (FF,), 0.5, 3.0, ((0, 4),), jnp.float32)
    w_down = bell_draw(key_list[10], (FF, D), FF ** -0.5, 0.0625, ((0, 4), (1, 8)))
    b_out = bell_draw(key_list[11], (D,), 0.5, 3.0, (), jnp.float32)
    cotangent = noise_with(key_list[12], (SEQS, LEN, D), 1.0, 6.0, ((0, 8), (1, 4)), (0, 2, 8, 2.0), jnp.float32)
    return {"x_in": x_in, "segments": segments, "positions": positions, "ln_gain": ln_gain, "ln_bias": ln_bias, "w_qkv": w_qkv, "b_qkv": b_qkv, "w_out": w_out, "w_up": w_up, "b_up": b_up, "w_down": w_down, "b_out": b_out, "cotangent": cotangent}


EPSILON = 1e-05
MASKED = -1e+30

def rotary_tables(places, rot_dims):
    half_rot = rot_dims // 2
    freqs = 10000.0 ** (-(jnp.arange(half_rot, dtype=jnp.float32) * 2.0 / rot_dims))
    angles = places.astype(jnp.float32)[:, None] * freqs[None, :]
    return (jnp.cos(angles)[:, None, :], jnp.sin(angles)[:, None, :])

def rotate(tensor, cosines, sines, rot_dims):
    half_rot = rot_dims // 2
    first = tensor[..., :half_rot]
    second = tensor[..., half_rot:rot_dims]
    return jnp.concatenate([first * cosines - second * sines, second * cosines + first * sines, tensor[..., rot_dims:]], -1)

def unrotate(tensor, cosines, sines, rot_dims):
    half_rot = rot_dims // 2
    first = tensor[..., :half_rot]
    second = tensor[..., half_rot:rot_dims]
    return jnp.concatenate([first * cosines + second * sines, second * cosines - first * sines, tensor[..., rot_dims:]], -1)

def allowed_mask(segment, lower, upper):
    places = jnp.arange(segment.shape[0])
    causal = places[None, :upper] <= places[lower:upper, None]
    same = segment[None, :upper] == segment[lower:upper, None]
    return causal & same

def attend(query, keys, values, segment, scale):
    length = query.shape[0]
    block = min(512, length)
    outputs = []
    logs = []
    for which in range(length // block):
        lower = which * block
        upper = lower + block
        scores = jnp.einsum('qhd,khd->hqk', query[lower:upper].astype(jnp.float32), keys[:upper].astype(jnp.float32)) * scale
        scores = jnp.where(allowed_mask(segment, lower, upper)[None], scores, MASKED)
        largest = lax.optimization_barrier(jnp.max(scores, -1, keepdims=True))
        raised = jnp.exp(scores - largest)
        totals = lax.optimization_barrier(jnp.sum(raised, -1, keepdims=True))
        probs = (raised / totals).astype(jnp.bfloat16)
        outputs.append(jnp.einsum('hqk,khd->qhd', probs.astype(jnp.float32), values[:upper].astype(jnp.float32)))
        logs.append((largest + jnp.log(totals))[..., 0])
    return (jnp.concatenate(outputs, 0), jnp.concatenate(logs, 1))

def attend_back(query, keys, values, segment, scale, attended, log_total, d_att):
    length = query.shape[0]
    block = min(512, length)
    d_keys = jnp.zeros(keys.shape, jnp.float32)
    d_values = jnp.zeros(values.shape, jnp.float32)
    pieces = []
    for which in range(length // block):
        lower = which * block
        upper = lower + block
        query_f = query[lower:upper].astype(jnp.float32)
        keys_f = keys[:upper].astype(jnp.float32)
        grad_f = d_att[lower:upper].astype(jnp.float32)
        scores = jnp.einsum('qhd,khd->hqk', query_f, keys_f) * scale
        scores = jnp.where(allowed_mask(segment, lower, upper)[None], scores, MASKED)
        probs = jnp.exp(scores - log_total[:, lower:upper, None])
        probs_bf = probs.astype(jnp.bfloat16).astype(jnp.float32)
        d_values = d_values.at[:upper].add(jnp.einsum('hqk,qhd->khd', probs_bf, grad_f))
        d_probs = jnp.einsum('qhd,khd->hqk', grad_f, values[:upper].astype(jnp.float32))
        delta = jnp.einsum('qhd,qhd->hq', grad_f, attended[lower:upper])
        d_scores = (probs * (d_probs - delta[..., None]) * scale).astype(jnp.bfloat16).astype(jnp.float32)
        pieces.append(jnp.einsum('hqk,khd->qhd', d_scores, keys_f))
        d_keys = d_keys.at[:upper].add(jnp.einsum('hqk,qhd->khd', d_scores, query_f))
    return (jnp.concatenate(pieces, 0), d_keys, d_values)

def one_sequence(x_rows, segment, places, dy_rows, ln_gain, ln_bias, w_qkv, b_qkv, w_out, w_up, b_up, w_down, b_out):
    length = x_rows.shape[0]
    scale = HD ** (-0.5)
    average = lax.optimization_barrier(jnp.mean(x_rows, -1, keepdims=True))
    centred = x_rows - average
    variance = lax.optimization_barrier(jnp.mean(centred * centred, -1, keepdims=True))
    inv_std = lax.rsqrt(variance + EPSILON)
    whitened = centred * inv_std
    normed = (whitened * ln_gain + ln_bias).astype(jnp.bfloat16)
    proj = jnp.dot(normed, w_qkv.reshape(D, 3 * D), preferred_element_type=jnp.float32).reshape(length, 3, D) + b_qkv[None]
    cosines, sines = rotary_tables(places, ROT)
    query = rotate(proj[:, 0].reshape(length, H, HD), cosines, sines, ROT).astype(jnp.bfloat16)
    keys = rotate(proj[:, 1].reshape(length, H, HD), cosines, sines, ROT).astype(jnp.bfloat16)
    values = proj[:, 2].reshape(length, H, HD).astype(jnp.bfloat16)
    attended, log_total = attend(query, keys, values, segment, scale)
    attended_bf = attended.reshape(length, D).astype(jnp.bfloat16)
    pre_act = jnp.dot(normed, w_up, preferred_element_type=jnp.float32) + b_up
    activ = jax.nn.gelu(pre_act, approximate=True).astype(jnp.bfloat16)
    branch = jnp.dot(attended_bf, w_out, preferred_element_type=jnp.float32) + jnp.dot(activ, w_down, preferred_element_type=jnp.float32)
    result = x_rows + branch + b_out
    grad_bf = dy_rows.astype(jnp.bfloat16)
    g_wo = jnp.dot(attended_bf.T, grad_bf, preferred_element_type=jnp.float32)
    d_att = jnp.dot(grad_bf, w_out.T, preferred_element_type=jnp.float32).astype(jnp.bfloat16).reshape(length, H, HD)
    g_wd = jnp.dot(activ.T, grad_bf, preferred_element_type=jnp.float32)
    d_act = jnp.dot(grad_bf, w_down.T, preferred_element_type=jnp.float32)
    _, gelu_back = jax.vjp(partial(jax.nn.gelu, approximate=True), pre_act)
    d_pre = gelu_back(d_act)[0]
    g_bu = lax.optimization_barrier(jnp.sum(d_pre, 0))
    d_pre_bf = d_pre.astype(jnp.bfloat16)
    g_wu = jnp.dot(normed.T, d_pre_bf, preferred_element_type=jnp.float32)
    d_normed = jnp.dot(d_pre_bf, w_up.T, preferred_element_type=jnp.float32)
    d_query, d_keys, d_values = attend_back(query, keys, values, segment, scale, attended, log_total, d_att)
    d_query = unrotate(d_query, cosines, sines, ROT)
    d_keys = unrotate(d_keys, cosines, sines, ROT)
    d_proj = jnp.stack([d_query.reshape(length, D), d_keys.reshape(length, D), d_values.reshape(length, D)], 1)
    g_bq = lax.optimization_barrier(jnp.sum(d_proj, 0))
    d_proj_bf = d_proj.reshape(length, 3 * D).astype(jnp.bfloat16)
    g_wq = jnp.dot(normed.T, d_proj_bf, preferred_element_type=jnp.float32).reshape(D, 3, D)
    d_normed = d_normed + jnp.dot(d_proj_bf, w_qkv.reshape(D, 3 * D).T, preferred_element_type=jnp.float32)
    g_gain = lax.optimization_barrier(jnp.sum(d_normed * whitened, 0))
    g_lnb = lax.optimization_barrier(jnp.sum(d_normed, 0))
    d_hat = d_normed * ln_gain
    d_x = inv_std * (d_hat - lax.optimization_barrier(jnp.mean(d_hat, -1, keepdims=True)) - whitened * lax.optimization_barrier(jnp.mean(d_hat * whitened, -1, keepdims=True)))
    x_grad = dy_rows + d_x
    g_bo = lax.optimization_barrier(jnp.sum(dy_rows, 0))
    return (result, x_grad, (g_gain, g_lnb, g_wq, g_bq, g_wo, g_wu, g_bu, g_wd, g_bo))

def reference(x_in, segments, positions, ln_gain, ln_bias, w_qkv, b_qkv, w_out, w_up, b_up, w_down, b_out, cotangent):
    zeros_init = (jnp.zeros((D,), jnp.float32), jnp.zeros((D,), jnp.float32), jnp.zeros((D, 3, D), jnp.float32), jnp.zeros((3, D), jnp.float32), jnp.zeros((D, D), jnp.float32), jnp.zeros((D, FF), jnp.float32), jnp.zeros((FF,), jnp.float32), jnp.zeros((FF, D), jnp.float32), jnp.zeros((D,), jnp.float32))

    def step(carry, inputs):
        x_rows, segment, places, dy_rows = inputs
        result, x_grad, grads = one_sequence(x_rows, segment, places, dy_rows, ln_gain, ln_bias, w_qkv, b_qkv, w_out, w_up, b_up, w_down, b_out)
        return (jax.tree.map(lambda total, term: total + term, carry, grads), (result, x_grad))
    totals, (result, x_grad) = lax.scan(step, zeros_init, (x_in, segments, positions, cotangent))
    g_gain, g_lnb, g_wq, g_bq, g_wo, g_wu, g_bu, g_wd, g_bo = totals
    return (result, x_grad, g_gain, g_lnb, g_wq, g_bq, g_wo, g_wu, g_bu, g_wd, g_bo)
```

```python
from functools import partial

import jax
import jax.numpy as jnp
from jax import lax
from jax.sharding import PartitionSpec as P

HD = 64
ROT = 32


EPSILON = 1e-05
MASKED = -1e30


def rotary_tables(places, rot_dims):
    half_rot = rot_dims // 2
    freqs = 10000.0 ** (-(jnp.arange(half_rot, dtype=jnp.float32) * 2.0 / rot_dims))
    angles = places.astype(jnp.float32)[:, None] * freqs[None, :]
    return (jnp.cos(angles)[:, None, :], jnp.sin(angles)[:, None, :])


def rotate(tensor, cosines, sines, rot_dims):
    half_rot = rot_dims // 2
    first = tensor[..., :half_rot]
    second = tensor[..., half_rot:rot_dims]
    return jnp.concatenate(
        [
            first * cosines - second * sines,
            second * cosines + first * sines,
            tensor[..., rot_dims:],
        ],
        -1,
    )


def unrotate(tensor, cosines, sines, rot_dims):
    half_rot = rot_dims // 2
    first = tensor[..., :half_rot]
    second = tensor[..., half_rot:rot_dims]
    return jnp.concatenate(
        [
            first * cosines + second * sines,
            second * cosines - first * sines,
            tensor[..., rot_dims:],
        ],
        -1,
    )


def allowed_mask(segment, lower, upper):
    places = jnp.arange(segment.shape[0])
    causal = places[None, :upper] <= places[lower:upper, None]
    same = segment[None, :upper] == segment[lower:upper, None]
    return causal & same


def inner_rows(left, right):
    return lax.dot_general(
        left, right, (((0,), (0,)), ((), ())), preferred_element_type=jnp.float32
    )


def times_transpose(left, right):
    return lax.dot_general(
        left, right, (((1,), (1,)), ((), ())), preferred_element_type=jnp.float32
    )


def attend(query, keys, values, segment, scale):
    length = query.shape[0]
    block = min(512, length)
    outputs = []
    logs = []
    for which in range(length // block):
        lower = which * block
        upper = lower + block
        scores = (
            jnp.einsum(
                "qhd,khd->hqk", query[lower:upper], keys[:upper], preferred_element_type=jnp.float32
            )
            * scale
        )
        scores = jnp.where(allowed_mask(segment, lower, upper)[None], scores, MASKED)
        largest = jnp.max(scores, -1, keepdims=True)
        raised = jnp.exp(scores - largest)
        totals = jnp.sum(raised, -1, keepdims=True)
        probs = (raised / totals).astype(jnp.bfloat16)
        outputs.append(
            jnp.einsum("hqk,khd->qhd", probs, values[:upper], preferred_element_type=jnp.float32)
        )
        logs.append((largest + jnp.log(totals))[..., 0])
    return (jnp.concatenate(outputs, 0), jnp.concatenate(logs, 1))


def attend_back(query, keys, values, segment, scale, attended, log_total, d_att):
    length = query.shape[0]
    block = min(512, length)
    d_keys = jnp.zeros(keys.shape, jnp.float32)
    d_values = jnp.zeros(values.shape, jnp.float32)
    pieces = []
    for which in range(length // block):
        lower = which * block
        upper = lower + block
        grad_block = d_att[lower:upper]
        scores = (
            jnp.einsum(
                "qhd,khd->hqk", query[lower:upper], keys[:upper], preferred_element_type=jnp.float32
            )
            * scale
        )
        scores = jnp.where(allowed_mask(segment, lower, upper)[None], scores, MASKED)
        probs = jnp.exp(scores - log_total[:, lower:upper, None])
        probs_bf = probs.astype(jnp.bfloat16)
        d_values = d_values.at[:upper].add(
            jnp.einsum("hqk,qhd->khd", probs_bf, grad_block, preferred_element_type=jnp.float32)
        )
        d_probs = jnp.einsum(
            "qhd,khd->hqk", grad_block, values[:upper], preferred_element_type=jnp.float32
        )
        delta = jnp.einsum("qhd,qhd->hq", grad_block.astype(jnp.float32), attended[lower:upper])
        d_scores = (probs * (d_probs - delta[..., None]) * scale).astype(jnp.bfloat16)
        pieces.append(
            jnp.einsum("hqk,khd->qhd", d_scores, keys[:upper], preferred_element_type=jnp.float32)
        )
        d_keys = d_keys.at[:upper].add(
            jnp.einsum(
                "hqk,qhd->khd", d_scores, query[lower:upper], preferred_element_type=jnp.float32
            )
        )
    return (jnp.concatenate(pieces, 0), d_keys, d_values)


def permute(value, axis, pairs):
    return lax.ppermute(value, axis, pairs)


def rows_of(array, start, count, axis=0):
    return lax.dynamic_slice_in_dim(array, start * count, count, axis)


class Places:
    def __init__(self, dp, tensor):
        self.outers = dp // 2
        self.dp_at = lax.axis_index("dp")
        self.outer, self.side = self.dp_at // 2, self.dp_at % 2
        tensor_at = lax.axis_index("tensor")
        self.far, self.core = tensor_at // 2, tensor_at % 2
        self.side_pairs = [(i, i ^ 1) for i in range(dp)]
        self.far_pairs = [(i, i ^ 2) for i in range(tensor)]
        self.core_pairs = [(i, i ^ 1) for i in range(tensor)]
        self.columns = [[o * 2 + s for o in range(self.outers)] for s in range(2)]

    def to_side(self, value):
        return permute(value, "dp", self.side_pairs)

    def to_far(self, value):
        return permute(value, "tensor", self.far_pairs)

    def to_core(self, value):
        return permute(value, "tensor", self.core_pairs)

    def by_side(self, own, other, axis):
        first = jnp.where(self.side == 0, own, other)
        second = jnp.where(self.side == 0, other, own)
        return jnp.concatenate([first, second], axis)


def gather_rows(block, at):
    rows, width = block.shape
    half = rows // 2
    from_side = at.to_side(block)
    from_far = at.to_far(block)
    top = at.to_side(from_far[:half])
    bottom = at.to_far(from_side[half:])
    whole = jnp.zeros((2, 2, 2, rows, width), block.dtype)

    def put(whole, value, side, far, core, offset=0):
        return lax.dynamic_update_slice(whole, value[None, None, None], (side, far, core, offset, 0))

    other = 1 - at.core
    for value, side, far, offset in (
        (block, at.side, at.far, 0),
        (from_side, 1 - at.side, at.far, 0),
        (from_far, at.side, 1 - at.far, 0),
        (top, 1 - at.side, 1 - at.far, 0),
        (bottom, 1 - at.side, 1 - at.far, half),
    ):
        whole = put(whole, value, side, far, at.core, offset)
        whole = put(whole, at.to_core(value), side, far, other, offset)
    return whole


def reduce_rows(partial, at):
    rows, width = partial.shape[3:]
    half = rows // 2

    def pick(array, side, far):
        return lax.dynamic_slice(array, (side, far, 0, 0), (1, 1, rows, width))[0, 0]

    def core_part(core):
        return lax.dynamic_slice(partial, (0, 0, core, 0, 0), (2, 2, 1, rows, width))[:, :, 0]

    def plus(a, b):
        return a.astype(jnp.float32) + b.astype(jnp.float32)

    received = at.to_core(core_part(1 - at.core))
    kept = plus(core_part(at.core), received).astype(jnp.bfloat16)
    diagonal = pick(kept, 1 - at.side, 1 - at.far)
    top = at.to_side(diagonal[:half])
    bottom = at.to_far(diagonal[half:])
    for_far = pick(kept, at.side, 1 - at.far)
    for_side = pick(kept, 1 - at.side, at.far)
    for_far = jnp.concatenate([plus(for_far[:half], top).astype(jnp.bfloat16), for_far[half:]], 0)
    for_side = jnp.concatenate([for_side[:half], plus(for_side[half:], bottom).astype(jnp.bfloat16)], 0)
    own = pick(kept, at.side, at.far)
    return plus(own, at.to_side(for_side)) + at.to_far(for_far).astype(jnp.float32)


def reduce_outer(grad, axis, at):
    outers = at.outers
    size = grad.shape[axis] // outers
    if outers != 4:
        return lax.psum_scatter(
            grad, "dp", scatter_dimension=axis, axis_index_groups=at.columns, tiled=True
        ).astype(jnp.float32)

    def pairs(links):
        return [(a * 2 + s, b * 2 + s) for a, b in links for s in range(2)]

    def plus(a, b):
        return a.astype(jnp.float32) + b.astype(jnp.float32)

    pair = at.outer // 2
    inner = at.outer % 2
    away = rows_of(grad, 1 - pair, 2 * size, axis)
    first = permute(away, "dp", pairs([(0, 1), (3, 2)]))
    away = plus(away, first).astype(jnp.bfloat16)
    second = permute(away, "dp", pairs([(1, 2), (2, 1)]))
    near = rows_of(grad, pair, 2 * size, axis)
    near = plus(near, second)
    third = permute(
        rows_of(near, 1 - inner, size, axis).astype(jnp.bfloat16),
        "dp",
        pairs([(0, 1), (1, 0), (2, 3), (3, 2)]),
    )
    return plus(rows_of(near, inner, size, axis), third)


def on_device(
    dp,
    tensor,
    x_in,
    segments,
    positions,
    ln_gain,
    ln_bias,
    w_qkv,
    b_qkv,
    w_out,
    w_up,
    b_up,
    w_down,
    b_out,
    cotangent,
):
    at = Places(dp, tensor)
    own_rows, width = x_in.shape[1:]
    length = segments.shape[1]
    rows = 2 * length
    scale = HD ** (-0.5)
    local_width = w_out.shape[0] // 2
    heads_here = local_width // HD
    hidden = w_up.shape[1] // 2
    parts = 2
    chunk = hidden // parts

    def gather_outer(piece, axis):
        return lax.all_gather(piece, "dp", axis=axis, axis_index_groups=at.columns, tiled=True)

    qkv_flat = jnp.transpose(w_qkv, (1, 0, 2))
    qkv_own = rows_of(qkv_flat, at.side, local_width, 2)
    qkv_got = at.to_side(rows_of(qkv_flat, 1 - at.side, local_width, 2))
    qkv_piece = at.by_side(qkv_own, qkv_got, 1)
    qkv_piece = jnp.transpose(qkv_piece, (1, 0, 2)).reshape(-1, 3 * local_width)
    wq = gather_outer(qkv_piece, 0)
    out_piece = at.by_side(
        rows_of(w_out, at.side, local_width), at.to_side(rows_of(w_out, 1 - at.side, local_width)), 1
    )
    wo = gather_outer(out_piece, 1)
    up_piece = at.by_side(
        rows_of(w_up, at.side, hidden, 1), at.to_side(rows_of(w_up, 1 - at.side, hidden, 1)), 0
    )
    down_piece = at.by_side(
        rows_of(w_down, at.side, hidden), at.to_side(rows_of(w_down, 1 - at.side, hidden)), 1
    )
    wu = [gather_outer(up_piece[:, i * chunk : (i + 1) * chunk], 0) for i in range(parts)]
    wd = [gather_outer(down_piece[i * chunk : (i + 1) * chunk], 1) for i in range(parts)]

    x_rows = x_in[0]
    average = jnp.mean(x_rows, -1, keepdims=True)
    centred = x_rows - average
    variance = jnp.mean(centred * centred, -1, keepdims=True)
    inv_std = lax.rsqrt(variance + EPSILON)
    whitened = centred * inv_std
    normed = (whitened * ln_gain + ln_bias).astype(jnp.bfloat16)
    full_normed = gather_rows(normed, at).reshape(rows, width)
    cot_rows = cotangent[0]
    full_grad = gather_rows(cot_rows.astype(jnp.bfloat16), at).reshape(rows, width)

    marks = jnp.concatenate([segments, positions], 0)
    marks = at.by_side(marks[None], at.to_side(marks)[None], 0)
    segment, places = marks[:, 0], marks[:, 1]
    b_qkv_own = rows_of(b_qkv, at.side, local_width, 1)
    b_up_own = rows_of(b_up, at.side, hidden)

    proj = jnp.dot(full_normed, wq, preferred_element_type=jnp.float32).reshape(
        rows, 3, local_width
    ) + b_qkv_own[None]
    cosines, sines = rotary_tables(places.reshape(rows), ROT)
    query = rotate(proj[:, 0].reshape(rows, heads_here, HD), cosines, sines, ROT).astype(jnp.bfloat16)
    keys = rotate(proj[:, 1].reshape(rows, heads_here, HD), cosines, sines, ROT).astype(jnp.bfloat16)
    values = proj[:, 2].reshape(rows, heads_here, HD).astype(jnp.bfloat16)
    d_att = times_transpose(full_grad, wo).astype(jnp.bfloat16).reshape(rows, heads_here, HD)
    outs, dqs, dks, dvs = [], [], [], []
    for s in range(2):
        span = slice(s * length, (s + 1) * length)
        out_part, log_part = attend(query[span], keys[span], values[span], segment[s], scale)
        dq, dk, dv = attend_back(
            query[span], keys[span], values[span], segment[s], scale, out_part, log_part, d_att[span]
        )
        outs.append(out_part)
        dqs.append(dq)
        dks.append(dk)
        dvs.append(dv)
    attended_bf = jnp.concatenate(outs, 0).reshape(rows, local_width).astype(jnp.bfloat16)
    d_query = unrotate(jnp.concatenate(dqs, 0), cosines, sines, ROT)
    d_keys = unrotate(jnp.concatenate(dks, 0), cosines, sines, ROT)
    d_proj = jnp.stack(
        [
            d_query.reshape(rows, local_width),
            d_keys.reshape(rows, local_width),
            jnp.concatenate(dvs, 0).reshape(rows, local_width),
        ],
        1,
    )
    g_bq = jnp.sum(d_proj, 0)
    d_proj_bf = d_proj.reshape(rows, 3 * local_width).astype(jnp.bfloat16)
    g_wo = reduce_outer(inner_rows(attended_bf, full_grad).astype(jnp.bfloat16), 1, at)
    g_wq = reduce_outer(inner_rows(full_normed, d_proj_bf).astype(jnp.bfloat16), 0, at)
    branch = jnp.dot(attended_bf, wo, preferred_element_type=jnp.float32)
    d_normed = times_transpose(d_proj_bf, wq)

    g_wu, g_wd, g_bu = [], [], []
    for i in range(parts):
        bias = b_up_own[i * chunk : (i + 1) * chunk]
        pre_act = jnp.dot(full_normed, wu[i], preferred_element_type=jnp.float32) + bias
        activ = jax.nn.gelu(pre_act, approximate=True).astype(jnp.bfloat16)
        g_wd.append(reduce_outer(inner_rows(activ, full_grad).astype(jnp.bfloat16), 1, at))
        branch = branch + jnp.dot(activ, wd[i], preferred_element_type=jnp.float32)
        d_act = times_transpose(full_grad, wd[i])
        _, gelu_back = jax.vjp(partial(jax.nn.gelu, approximate=True), pre_act)
        d_pre = gelu_back(d_act)[0]
        g_bu.append(jnp.sum(d_pre, 0))
        d_pre_bf = d_pre.astype(jnp.bfloat16)
        g_wu.append(reduce_outer(inner_rows(full_normed, d_pre_bf).astype(jnp.bfloat16), 0, at))
        d_normed = d_normed + times_transpose(d_pre_bf, wu[i])

    shape = (2, 2, 2, own_rows, width)
    summed = reduce_rows(branch.astype(jnp.bfloat16).reshape(shape), at)
    result = x_rows + summed + b_out
    d_rows = reduce_rows(d_normed.astype(jnp.bfloat16).reshape(shape), at)
    g_gain = jnp.sum(d_rows * whitened, 0)
    g_lnb = jnp.sum(d_rows, 0)
    d_hat = d_rows * ln_gain
    d_x = inv_std * (
        d_hat
        - jnp.mean(d_hat, -1, keepdims=True)
        - whitened * jnp.mean(d_hat * whitened, -1, keepdims=True)
    )
    x_grad = cot_rows + d_x
    g_bo = jnp.sum(cot_rows, 0)

    def swap_back(grad, cut, join):
        size = grad.shape[cut] // 2
        own = rows_of(grad, at.side, size, cut)
        got = at.to_side(rows_of(grad, 1 - at.side, size, cut).astype(jnp.bfloat16))
        return at.by_side(own, got.astype(jnp.float32), join)

    g_wq = swap_back(g_wq.reshape(-1, 3, local_width), 0, 2)
    g_wo = swap_back(g_wo, 1, 0)
    g_wu = swap_back(jnp.concatenate(g_wu, 1), 0, 1)
    g_wd = swap_back(jnp.concatenate(g_wd, 0), 1, 0)

    def sided(value, axis):
        zero = jnp.zeros_like(value)
        return at.by_side(value, zero, axis)

    g_gain, g_lnb, g_bo = lax.psum((g_gain, g_lnb, g_bo), ("dp", "tensor"))
    g_bq, g_bu = lax.psum((sided(g_bq, 1), sided(jnp.concatenate(g_bu, 0), 0)), "dp")
    return (result[None], x_grad[None], g_gain, g_lnb, g_wq, g_bq, g_wo, g_wu, g_bu, g_wd, g_bo)


def solution(mesh):
    placed = (
        P("dp", "tensor", None),
        P("dp", None),
        P("dp", None),
        P(),
        P(),
        P("dp", None, "tensor"),
        P(None, "tensor"),
        P("tensor", "dp"),
        P("dp", "tensor"),
        P("tensor"),
        P("tensor", "dp"),
        P(),
        P("dp", "tensor", None),
    )
    return jax.shard_map(
        partial(on_device, mesh.shape["dp"], mesh.shape["tensor"]),
        mesh=mesh,
        in_specs=placed,
        out_specs=(
            P("dp", "tensor", None),
            P("dp", "tensor", None),
            P(),
            P(),
            P("dp", None, "tensor"),
            P(None, "tensor"),
            P("tensor", "dp"),
            P("dp", "tensor"),
            P("tensor"),
            P("tensor", "dp"),
            P(),
        ),
        check_vma=False,
    )
```
